32 devices in a mesh: curve: 4 (over x, core), group: 8 (over z, y).
Axes of the slice: x: 2, y: 2, z: 4, core: 2. Of those that a mesh axis runs over, the one named last changes fastest.
Arguments:
- composition: float32 [1536, 53, 256], P(('curve', 'group')), may hold values from -4 to 4
- heat_level: float32 [1536, 256], P(('curve', 'group')), may hold values from 1000 to 2500
- step_counts: int32 [1536], P(('curve', 'group')), may hold values from 1 to 3
- burning_parcel_roster: int32 [192], P(('curve', 'group')), may hold values from 0 to 47, as said below
- target_compute_place: int32 [192], P(('curve', 'group')), may hold values from -1 to 95, as said below
- partial_reciprocal_operator: float32 [192, 53, 53], P(('curve', 'group')), may hold values from -0.03 to 0.13
- speed_log_prefactor: float32 [268], replicated, may hold values from -1 to 1
- arrhenius_barrier: float32 [268], replicated, may hold values from 0.5 to 4
- leading_ingredient: float32 [268, 53], replicated, may hold values from -0.875 to 0.875
- trailing_ingredient: float32 [268, 53], replicated, may hold values from -0.875 to 0.875
- molar_coefficients: float32 [53, 268], replicated, may hold values from -0.375 to 0.375
Outputs:
- new_species: float32 [1536, 53, 256], P(('curve', 'group'))
The draws below stay inside these ranges and needn't reach their ends.
Inputs may be any that keep to these rules, and one draw needn't show every extreme that they name: `burning_parcel_roster`: each owner's 6 entries name distinct blocks among its own 48 blocks. `target_compute_place`: -1 marks an entry that does not react; an owner's reacting entries come first in its list, and an owner has 0 to 6 of them. A value g sends the block to compute slot g % 3 of device g // 3, devices numbered with curve slowest; that device has the owner's curve index. Every value 0 to 95 appears exactly once, so each device integrates exactly 3 blocks; one owner sends at most 1 block to one device, and in every curve row some owner has 6 reacting entries and some owner has none.
All inputs are finite; a program needn't handle non-finite values.
Results may differ from the reference program's by a relative error of at most 0.0003.
Values sent between devices are 32-bit elements; how exact they have to be, the bound alone decides.
A program may use at most 64 MiB of HBM per device.

```python
import math
import jax
import jax.numpy as jnp
from jax import lax

S = 53
R = 268
PARCEL_VOLUMES = 256
SUBS = 3
MAXIN = 3
BLK_DEV = 48
LIST = 6
OWNERS = 32
PARCEL_COUNT = 1536
N_GROUP = 8


def draw_burning_parcel_roster(key, part):
    owner_keys = jax.random.split(jax.random.fold_in(key, 11), OWNERS)
    chosen = jax.vmap(lambda single: jax.random.permutation(single, BLK_DEV)[:LIST])(owner_keys)
    return chosen.reshape(-1).astype(jnp.int32)


def draw_target_compute_place(key, part):
    order_key, shift_key, device_key, slot_key, owner_key = jax.random.split(jax.random.fold_in(key, 23), 5)
    row_count = OWNERS // N_GROUP
    row_number = jnp.arange(row_count, dtype=jnp.int32)
    pairing = jax.vmap(lambda number: jax.random.permutation(jax.random.fold_in(order_key, number), N_GROUP))(row_number).astype(jnp.int32)
    shifts = jax.random.randint(shift_key, (row_count, N_GROUP // 2), 0, MAXIN + 1).astype(jnp.int32)
    shifts = shifts.at[:, 0].set(MAXIN)
    counts = jnp.full((row_count, N_GROUP), MAXIN, jnp.int32)
    counts = counts.at[row_number[:, None], pairing[:, 0::2]].add(shifts)
    counts = counts.at[row_number[:, None], pairing[:, 1::2]].add(-shifts)
    owner_order = jax.vmap(lambda number: jax.random.permutation(jax.random.fold_in(owner_key, number), N_GROUP))(row_number).astype(jnp.int32)
    walked = jnp.take_along_axis(counts, owner_order, axis=1)
    passed = jnp.cumsum(walked, axis=1) - walked
    starts = jnp.zeros((row_count, N_GROUP), jnp.int32).at[row_number[:, None], owner_order].set(passed)
    position = jnp.arange(LIST, dtype=jnp.int32)
    ordinal = starts[:, :, None] + position[None, None, :]
    device_map = jax.vmap(lambda number: jax.random.permutation(jax.random.fold_in(device_key, number), N_GROUP))(row_number).astype(jnp.int32)
    local_device = jnp.take_along_axis(device_map, (ordinal % N_GROUP).reshape(row_count, -1), axis=1).reshape(row_count, N_GROUP, LIST)
    device = row_number[:, None, None] * N_GROUP + local_device
    slot_maps = jax.vmap(lambda number: jax.random.permutation(jax.random.fold_in(slot_key, number), MAXIN))(jnp.arange(OWNERS)).astype(jnp.int32)
    slot_number = slot_maps[device, jnp.minimum(ordinal // N_GROUP, MAXIN - 1)]
    reacts = position[None, None, :] < counts[:, :, None]
    return jnp.where(reacts, device * MAXIN + slot_number, -1).reshape(-1).astype(jnp.int32)


def draw_partial_reciprocal_operator(key, part):
    spread = 0.5 / math.sqrt(S)
    full_shape = (OWNERS * LIST, S, S)
    perturb = jnp.clip(jax.random.normal(key, full_shape, jnp.float32) * spread, -0.3, 0.3)
    return 0.1 * (jnp.eye(S, dtype=jnp.float32)[None] + perturb)


def with_ends(array, own_key, smallest, top_value):
    place = [jax.random.randint(jax.random.fold_in(own_key, axis), (), 0, length) for axis, length in enumerate(array.shape)]
    widest = array.shape.index(max(array.shape))
    next_to = place[:widest] + [(place[widest] + 1) % array.shape[widest]] + place[widest + 1:]
    return array.at[tuple(place)].set(smallest).at[tuple(next_to)].set(top_value)


def levels(rng, dims, pieces, low, high):
    level = 1.0
    for dim, blocks in pieces:
        draws = jax.random.uniform(jax.random.fold_in(jax.random.fold_in(rng, 6), dim), (blocks,), jnp.float32, low / len(pieces), high / len(pieces))
        level = level * jnp.repeat(jnp.exp(draws), dims[dim] // blocks).reshape((-1,) + (1,) * (len(dims) - 1 - dim))
    return level


def normal_values(stream_key, dims, scale, reach, cuts=(), held_as=jnp.bfloat16):
    values = scale * jax.random.normal(stream_key, dims, jnp.float32)
    if cuts:
        values = values * levels(stream_key, dims, cuts, -0.22, 0.18)
    return jnp.clip(values, -reach, reach).astype(held_as)


def setup_inputs(seed: int = 0) -> dict:
    streams_of = jax.random.split(jax.random.key(seed), 12)
    composition = normal_values(streams_of[0], (PARCEL_COUNT, S, PARCEL_VOLUMES), 1.0, 4.0, ((0, 32),), jnp.float32)
    heat_level = jnp.clip(1000.0 + 1500.0 * jax.random.uniform(streams_of[1], (PARCEL_COUNT, PARCEL_VOLUMES), jnp.float32) ** levels(streams_of[1], (PARCEL_COUNT, PARCEL_VOLUMES), ((0, 32),), -0.2, 0.2), 1000.0, 2500.0)
    step_counts = with_ends(jax.random.randint(streams_of[2], (PARCEL_COUNT,), 1, SUBS + 1), jax.random.fold_in(streams_of[2], 1), 1, SUBS).astype(jnp.int32)
    burning_parcel_roster = draw_burning_parcel_roster(jax.random.fold_in(streams_of[11], 71), 0)
    target_compute_place = draw_target_compute_place(jax.random.fold_in(streams_of[11], 71), 0)
    partial_reciprocal_operator = draw_partial_reciprocal_operator(jax.random.fold_in(streams_of[11], 71), 0)
    speed_log_prefactor = jnp.clip(jax.random.uniform(streams_of[6], (R,), jnp.float32, -1.0, 1.0), -1.0, 1.0)
    arrhenius_barrier = jnp.clip(jnp.exp(jax.random.uniform(streams_of[7], (R,), jnp.float32, math.log(0.5), math.log(4.0))), 0.5, 4.0)
    leading_ingredient = normal_values(streams_of[8], (R, S), S ** -0.5, 0.875, (), jnp.float32)
    trailing_ingredient = normal_values(streams_of[9], (R, S), S ** -0.5, 0.875, (), jnp.float32)
    molar_coefficients = normal_values(streams_of[10], (S, R), R ** -0.5, 0.375, (), jnp.float32)
    return {"composition": composition, "heat_level": heat_level, "step_counts": step_counts, "burning_parcel_roster": burning_parcel_roster, "target_compute_place": target_compute_place, "partial_reciprocal_operator": partial_reciprocal_operator, "speed_log_prefactor": speed_log_prefactor, "arrhenius_barrier": arrhenius_barrier, "leading_ingredient": leading_ingredient, "trailing_ingredient": trailing_ingredient, "molar_coefficients": molar_coefficients}


step_size = 0.2
section_shift = (2.0, 1.92, 0.24)
section_couple = (-8.0, 14.88, 2.4, -0.896, -0.432, -0.4)
section_weight = (19.0 / 9.0, 0.5, 25.0 / 108.0, 125.0 / 108.0)


def kinetic_speed_coefficients(heat_level, speed_log_prefactor, arrhenius_barrier):
    reciprocal_operator = 1000.0 / heat_level
    return jnp.exp(speed_log_prefactor[None, :, None] - arrhenius_barrier[None, :, None] * (reciprocal_operator[:, None, :] - 0.6))


def net_rates(present_composition, kinetic_speed_coefficient, reactants, molar_coefficients):
    paired = jnp.einsum("rs,msc->mrc", reactants, present_composition, precision=lax.Precision.HIGHEST)
    reaction_count = kinetic_speed_coefficient.shape[1]
    progress = kinetic_speed_coefficient * paired[:, :reaction_count] * paired[:, reaction_count:]
    return jnp.einsum("sr,mrc->msc", molar_coefficients, progress, precision=lax.Precision.HIGHEST)


def apply_matrix(matrix, vector):
    return jnp.einsum("mst,mtc->msc", matrix, vector, precision=lax.Precision.HIGHEST)


def advance_partial_step(present_composition, heat_level, step_counts, partial_reciprocal_operator, speed_log_prefactor, arrhenius_barrier, leading_ingredient, trailing_ingredient, molar_coefficients):
    reactants = jnp.concatenate([leading_ingredient, trailing_ingredient], axis=0)
    kinetic_speed_coefficient = kinetic_speed_coefficients(heat_level, speed_log_prefactor, arrhenius_barrier)
    weights = step_counts.astype(jnp.float32)
    per_step = (weights / step_size)[:, None, None]
    scaled = partial_reciprocal_operator / weights[:, None, None]
    for substep in range(SUBS):
        rates_one = net_rates(present_composition, kinetic_speed_coefficient, reactants, molar_coefficients)
        section_one = apply_matrix(scaled, rates_one)
        point_two = present_composition + section_shift[0] * section_one
        rates_two = net_rates(point_two, kinetic_speed_coefficient, reactants, molar_coefficients)
        section_two = apply_matrix(scaled, rates_two + section_couple[0] * per_step * section_one)
        point_three = present_composition + section_shift[1] * section_one + section_shift[2] * section_two
        rates_three = net_rates(point_three, kinetic_speed_coefficient, reactants, molar_coefficients)
        section_three = apply_matrix(scaled, rates_three + per_step * (section_couple[1] * section_one + section_couple[2] * section_two))
        section_four = apply_matrix(scaled, rates_three + per_step * (section_couple[3] * section_one + section_couple[4] * section_two + section_couple[5] * section_three))
        advanced = present_composition + section_weight[0] * section_one + section_weight[1] * section_two + section_weight[2] * section_three + section_weight[3] * section_four
        active = (substep < step_counts)[:, None, None]
        present_composition = jnp.where(active, advanced, present_composition)
    return present_composition


def reference(composition, heat_level, step_counts, burning_parcel_roster, target_compute_place, partial_reciprocal_operator, speed_log_prefactor, arrhenius_barrier, leading_ingredient, trailing_ingredient, molar_coefficients):
    entries = jnp.arange(OWNERS * LIST, dtype=jnp.int32)
    owner_of = entries // LIST
    global_block = (owner_of * BLK_DEV + burning_parcel_roster).astype(jnp.int32)
    reacts = target_compute_place >= 0
    slot_total = OWNERS * MAXIN
    target = jnp.where(reacts, target_compute_place, slot_total).astype(jnp.int32)
    sending_holder = jnp.zeros((slot_total,), jnp.int32).at[target].set(entries, mode="drop")
    slot_block = global_block[sending_holder]

    def run_device(indices):
        parcel_line_operator, item_line_operator = indices
        return advance_partial_step(composition[parcel_line_operator], heat_level[parcel_line_operator], step_counts[parcel_line_operator], partial_reciprocal_operator[item_line_operator], speed_log_prefactor, arrhenius_barrier, leading_ingredient, trailing_ingredient, molar_coefficients)

    finished = lax.map(run_device, (slot_block.reshape(OWNERS, MAXIN), sending_holder.reshape(OWNERS, MAXIN)))
    finished = finished.reshape((slot_total,) + composition.shape[1:])
    return composition.at[slot_block].set(finished)
```

```python
import jax
import jax.numpy as jnp
from jax import lax
from jax.experimental import pallas as pl
from jax.experimental.pallas import tpu as pltpu
from jax.sharding import PartitionSpec as P

SUBS = 3
STREAMS = 2

F32 = jnp.float32
BF16 = jnp.bfloat16


def up(n, m):
    return (n + m - 1) // m * m


def dot32(a, b):
    return jnp.dot(a, b, preferred_element_type=F32)


def split(v):
    hi = v.astype(BF16)
    return hi, (v - hi.astype(F32)).astype(BF16)


def make_kernel(species, reactions, blocks, cells, listed):
    sp = up(species, 64)
    rp = up(reactions, 16)
    main = reactions // 128 * 128
    tail = rp - main
    wide = 2 * main + 256

    def kernel(
        comp, heat, counts, roster, target, inverse, pref, barr, lead, trail, molar,
        out,
        bulk, ybuf, y, kf, w_ref, n_ref, a_ref, call, cols, stage, units, sem_in, sem_out, sem_y,
    ):
        big_in = pltpu.make_async_copy(comp, bulk, sem_in)
        big_out = pltpu.make_async_copy(bulk, out, sem_out)

        def reacts(e):
            return target[e] >= 0

        def fetch(e):
            return pltpu.make_async_copy(comp.at[:, roster[e], :], ybuf.at[e], sem_y.at[e])

        def deliver(e):
            return pltpu.make_async_copy(ybuf.at[e], out.at[:, roster[e], :], sem_y.at[e])

        for e in range(listed):
            @pl.when(reacts(e))
            def _():
                fetch(e).start()
        big_in.start()

        total = jnp.int32(0)
        longest = jnp.int32(0)
        for i in range(units.shape[0]):
            units[i] = listed
        for e in range(listed):
            w = jnp.where(reacts(e), counts[roster[e]], 0)
            for k in range(SUBS):
                @pl.when(k < w)
                def _(total=total, k=k, e=e):
                    units[total + k] = e
            total = total + w
            longest = jnp.maximum(longest, w)
        trips = jnp.maximum((total + STREAMS - 1) // STREAMS, longest)

        y[listed] = jnp.zeros((sp, cells), F32)
        kf[listed] = jnp.zeros((rp, cells), F32)
        w_ref[listed] = jnp.zeros((2 * sp, wide), BF16)
        n_ref[listed] = jnp.zeros((2 * sp, 2 * sp), BF16)

        for i, part in enumerate((lead, trail)):
            stage[...] = jnp.zeros(stage.shape, F32)
            stage[0:species, 0:reactions] = part[...]
            full = stage[...]
            hi = full.astype(BF16).astype(F32)
            lo = full - hi
            turned = jnp.concatenate([hi, hi, lo, lo], axis=0).T
            a_ref[pl.ds(i * rp, rp), :] = turned[0:rp].astype(BF16)
        stage[...] = jnp.zeros(stage.shape, F32)
        stage[0:species, 0:reactions] = molar[...]
        call[:, 0:main] = stage[:, 0:main]
        call[:, main:2 * main] = stage[:, 0:main]
        row = lax.broadcasted_iota(jnp.int32, (sp, 256), 0)
        col = lax.broadcasted_iota(jnp.int32, (sp, 256), 1) - 2 * tail
        eye = jnp.where((col == row) | (col == row + sp), 5.0, 0.0).astype(F32)
        rest = stage[:, main:main + 128]
        rest = rest + pltpu.roll(rest, tail, 1)
        call[:, 2 * main:2 * main + 256] = eye + jnp.concatenate(
            [rest, jnp.zeros_like(rest)], axis=1
        )
        stage[...] = jnp.zeros(stage.shape, F32)
        stage[0:1, 0:reactions] = pref[...].reshape(1, reactions)
        stage[1:2, 0:reactions] = barr[...].reshape(1, reactions)
        turned = stage[...].T
        cols[0] = jnp.broadcast_to(turned[0:rp, 0:1], (rp, cells))
        cols[1] = jnp.broadcast_to(turned[0:rp, 1:2], (rp, cells))

        big_in.wait()
        big_out.start()

        lane = lax.broadcasted_iota(jnp.int32, (1, wide), 1)
        coupled = (lane >= 2 * main + 2 * tail)

        def prepare(e, carry):
            @pl.when(reacts(e))
            def _():
                b = roster[e]
                weight = counts[b].astype(F32)
                warm = 1000.0 / heat[pl.ds(b, 1), :] - 0.6
                kf[e] = jnp.exp(cols[0] - cols[1] * warm)
                stage[:, 0:128] = jnp.zeros((sp, 128), F32)
                stage[0:species, 0:species] = inverse[e]
                scaled = jnp.dot(
                    stage[:, 0:sp], call[...],
                    precision=lax.Precision.HIGHEST, preferred_element_type=F32,
                )
                scaled = jnp.where(coupled, scaled, scaled / weight)
                hi, lo = split(scaled)
                w_ref[e, 0:sp, :] = hi
                w_ref[e, sp:2 * sp, :] = lo
                hi, lo = split(stage[:, 0:sp] * 5.0)
                n_ref[e, 0:sp, :] = jnp.concatenate([hi, hi], axis=1)
                n_ref[e, sp:2 * sp, :] = jnp.concatenate([lo, lo], axis=1)
                fetch(e).wait()
                y[e] = jnp.zeros((sp, cells), F32)
                y[e, 0:species, :] = ybuf[e]
            return carry

        lax.fori_loop(0, listed, prepare, 0)

        def fold(o):
            return o[0:sp] + o[sp:2 * sp]

        def rates(v, e):
            x1, x2 = split(v)
            z = dot32(a_ref[...], jnp.concatenate([x1, x2, x1, x2], axis=0))
            return split(kf[e] * z[0:rp] * z[rp:2 * rp])

        def section(p, e, u=None):
            p1, p2 = p
            parts = [p1[0:main], p2[0:main], p1[main:rp], p2[main:rp]]
            if u is not None:
                parts += list(split(u))
            rhs = jnp.concatenate(parts, axis=0)
            return fold(dot32(w_ref[e, :, 0:rhs.shape[0]], rhs))

        def couple(e, u):
            return fold(dot32(n_ref[e], jnp.concatenate(list(split(u)), axis=0)))

        def step(i, carry):
            es = [units[i + s * trips] for s in range(STREAMS)]
            y0 = [y[e] for e in es]
            p = [rates(v, e) for v, e in zip(y0, es)]
            g1 = [section(a, e) for a, e in zip(p, es)]
            p = [rates(v + 2.0 * g, e) for v, g, e in zip(y0, g1, es)]
            g2 = [section(a, e, -8.0 * g) for a, g, e in zip(p, g1, es)]
            p = [rates(v + 1.92 * a + 0.24 * b, e) for v, a, b, e in zip(y0, g1, g2, es)]
            g3 = [section(q, e, 14.88 * a + 2.4 * b) for q, a, b, e in zip(p, g1, g2, es)]
            g4 = [
                c + couple(e, -15.776 * a - 2.832 * b - 0.4 * c)
                for a, b, c, e in zip(g1, g2, g3, es)
            ]
            for v, a, b, c, d, e in zip(y0, g1, g2, g3, g4, es):
                y[e] = (
                    v + (19.0 / 9.0) * a + 0.5 * b + (25.0 / 108.0) * c + (125.0 / 108.0) * d
                )
            return carry

        lax.fori_loop(0, trips, step, 0)

        big_out.wait()
        for e in range(listed):
            @pl.when(reacts(e))
            def _():
                ybuf[e] = y[e, 0:species, :]
                deliver(e).start()
        for e in range(listed):
            @pl.when(reacts(e))
            def _():
                deliver(e).wait()

    scratch = [
        pltpu.VMEM((species, blocks, cells), F32),
        pltpu.VMEM((listed, species, cells), F32),
        pltpu.VMEM((listed + 1, sp, cells), F32),
        pltpu.VMEM((listed + 1, rp, cells), F32),
        pltpu.VMEM((listed + 1, 2 * sp, wide), BF16),
        pltpu.VMEM((listed + 1, 2 * sp, 2 * sp), BF16),
        pltpu.VMEM((2 * rp, 4 * sp), BF16),
        pltpu.VMEM((sp, wide), F32),
        pltpu.VMEM((2, rp, cells), F32),
        pltpu.VMEM((sp, up(reactions, 128)), F32),
        pltpu.SMEM((STREAMS * listed * SUBS + STREAMS * SUBS,), jnp.int32),
        pltpu.SemaphoreType.DMA,
        pltpu.SemaphoreType.DMA,
        pltpu.SemaphoreType.DMA((listed,)),
    ]
    return kernel, scratch


def on_device(
    composition,
    heat_level,
    step_counts,
    burning_parcel_roster,
    target_compute_place,
    partial_reciprocal_operator,
    speed_log_prefactor,
    arrhenius_barrier,
    leading_ingredient,
    trailing_ingredient,
    molar_coefficients,
):
    blocks, species, cells = composition.shape
    reactions = speed_log_prefactor.shape[0]
    listed = burning_parcel_roster.shape[0]
    kernel, scratch = make_kernel(species, reactions, blocks, cells, listed)
    hbm = pl.BlockSpec(memory_space=pl.ANY)
    vmem = pl.BlockSpec(memory_space=pltpu.VMEM)
    smem = pl.BlockSpec(memory_space=pltpu.SMEM)
    out = pl.pallas_call(
        kernel,
        out_shape=jax.ShapeDtypeStruct((species, blocks, cells), composition.dtype),
        in_specs=[hbm, vmem, smem, smem, smem, vmem, vmem, vmem, vmem, vmem, vmem],
        out_specs=hbm,
        scratch_shapes=scratch,
        compiler_params=pltpu.CompilerParams(vmem_limit_bytes=40 * 1024 * 1024),
        name="integrate",
    )(
        jnp.transpose(composition, (1, 0, 2)),
        heat_level,
        step_counts,
        burning_parcel_roster,
        target_compute_place,
        partial_reciprocal_operator,
        speed_log_prefactor,
        arrhenius_barrier,
        leading_ingredient.T,
        trailing_ingredient.T,
        molar_coefficients,
    )
    return jnp.transpose(out, (1, 0, 2))


def solution(mesh):
    owners = tuple(mesh.axis_names)
    return jax.shard_map(
        on_device,
        mesh=mesh,
        in_specs=(
            P(owners, None, None),
            P(owners, None),
            P(owners),
            P(owners),
            P(owners),
            P(owners, None, None),
            P(),
            P(),
            P(),
            P(),
            P(),
        ),
        out_specs=P(owners, None, None),
        check_vma=False,
    )
```

```python
import jax
import jax.numpy as jnp
from jax import lax
from jax.experimental import pallas as pl
from jax.experimental.pallas import tpu as pltpu
from jax.sharding import PartitionSpec as P

SUBS = 3
STREAMS = 2

F32 = jnp.float32
BF16 = jnp.bfloat16


def up(n, m):
    return (n + m - 1) // m * m


def dot32(a, b):
    return jnp.dot(a, b, preferred_element_type=F32)


def split(v):
    hi = v.astype(BF16)
    return hi, (v - hi.astype(F32)).astype(BF16)


def make_kernel(species, reactions, blocks, cells, listed):
    sp = up(species, 64)
    rp = up(reactions, 16)
    main = reactions // 128 * 128
    tail = rp - main
    wide = 2 * main + 256

    def kernel(
        comp, heat_at, counts_at, roster_at, target_at, inverse_at, pref_at, barr_at, lead_at,
        trail_at, molar_at,
        out,
        bulk, ybuf, y, kf, w_ref, n_ref, a_ref, call, cols, stage, units,
        heat, counts, roster, target, inverse, pref, barr, lead, trail, molar,
        sem_in, sem_out, sem_y, sem_a,
    ):
        loads = [
            pltpu.make_async_copy(src, dst, sem_a.at[i])
            for i, (src, dst) in enumerate((
                (roster_at, roster), (target_at, target), (counts_at, counts),
                (lead_at, lead), (trail_at, trail), (pref_at, pref), (barr_at, barr),
                (molar_at, molar), (heat_at, heat), (inverse_at, inverse),
            ))
        ]
        for load in loads:
            load.start()
        big_in = pltpu.make_async_copy(comp, bulk, sem_in)
        big_out = pltpu.make_async_copy(bulk, out, sem_out)

        def reacts(e):
            return target[e] >= 0

        def fetch(e):
            return pltpu.make_async_copy(comp.at[:, roster[e], :], ybuf.at[e], sem_y.at[e])

        def deliver(e):
            return pltpu.make_async_copy(ybuf.at[e], out.at[:, roster[e], :], sem_y.at[e])

        big_in.start()
        for load in loads[:3]:
            load.wait()
        for e in range(listed):
            @pl.when(reacts(e))
            def _():
                fetch(e).start()

        total = jnp.int32(0)
        longest = jnp.int32(0)
        for i in range(units.shape[0]):
            units[i] = listed
        for e in range(listed):
            w = jnp.where(reacts(e), counts[roster[e]], 0)
            for k in range(SUBS):
                @pl.when(k < w)
                def _(total=total, k=k, e=e):
                    units[total + k] = e
            total = total + w
            longest = jnp.maximum(longest, w)
        trips = jnp.maximum((total + STREAMS - 1) // STREAMS, longest)

        y[listed] = jnp.zeros((sp, cells), F32)
        kf[listed] = jnp.zeros((rp, cells), F32)
        w_ref[listed] = jnp.zeros((2 * sp, wide), BF16)
        n_ref[listed] = jnp.zeros((2 * sp, 2 * sp), BF16)

        for load in loads[3:]:
            load.wait()
        for i, part in enumerate((lead, trail)):
            stage[...] = jnp.zeros(stage.shape, F32)
            stage[0:species, 0:reactions] = part[...]
            full = stage[...]
            hi = full.astype(BF16).astype(F32)
            lo = full - hi
            turned = jnp.concatenate([hi, hi, lo, lo], axis=0).T
            a_ref[pl.ds(i * rp, rp), :] = turned[0:rp].astype(BF16)
        stage[...] = jnp.zeros(stage.shape, F32)
        stage[0:species, 0:reactions] = molar[...]
        call[:, 0:main] = stage[:, 0:main]
        call[:, main:2 * main] = stage[:, 0:main]
        row = lax.broadcasted_iota(jnp.int32, (sp, 256), 0)
        col = lax.broadcasted_iota(jnp.int32, (sp, 256), 1) - 2 * tail
        eye = jnp.where((col == row) | (col == row + sp), 5.0, 0.0).astype(F32)
        rest = stage[:, main:main + 128]
        rest = rest + pltpu.roll(rest, tail, 1)
        call[:, 2 * main:2 * main + 256] = eye + jnp.concatenate(
            [rest, jnp.zeros_like(rest)], axis=1
        )
        stage[...] = jnp.zeros(stage.shape, F32)
        stage[0:1, 0:reactions] = pref[...].reshape(1, reactions)
        stage[1:2, 0:reactions] = barr[...].reshape(1, reactions)
        turned = stage[...].T
        cols[0] = jnp.broadcast_to(turned[0:rp, 0:1], (rp, cells))
        cols[1] = jnp.broadcast_to(turned[0:rp, 1:2], (rp, cells))

        big_in.wait()
        big_out.start()

        lane = lax.broadcasted_iota(jnp.int32, (1, wide), 1)
        coupled = (lane >= 2 * main + 2 * tail)

        def prepare(e, carry):
            @pl.when(reacts(e))
            def _():
                b = roster[e]
                weight = counts[b].astype(F32)
                warm = 1000.0 / heat[pl.ds(b, 1), :] - 0.6
                kf[e] = jnp.exp(cols[0] - cols[1] * warm)
                stage[:, 0:128] = jnp.zeros((sp, 128), F32)
                stage[0:species, 0:species] = inverse[e]
                scaled = jnp.dot(
                    stage[:, 0:sp], call[...],
                    precision=lax.Precision.HIGHEST, preferred_element_type=F32,
                )
                scaled = jnp.where(coupled, scaled, scaled / weight)
                hi, lo = split(scaled)
                w_ref[e, 0:sp, :] = hi
                w_ref[e, sp:2 * sp, :] = lo
                hi, lo = split(stage[:, 0:sp] * 5.0)
                n_ref[e, 0:sp, :] = jnp.concatenate([hi, hi], axis=1)
                n_ref[e, sp:2 * sp, :] = jnp.concatenate([lo, lo], axis=1)
                fetch(e).wait()
                y[e] = jnp.zeros((sp, cells), F32)
                y[e, 0:species, :] = ybuf[e]
            return carry

        lax.fori_loop(0, listed, prepare, 0)

        def fold(o):
            return o[0:sp] + o[sp:2 * sp]

        def rates(v, e):
            x1, x2 = split(v)
            z = dot32(a_ref[...], jnp.concatenate([x1, x2, x1, x2], axis=0))
            return split(kf[e] * z[0:rp] * z[rp:2 * rp])

        def section(p, e, u=None):
            p1, p2 = p
            parts = [p1[0:main], p2[0:main], p1[main:rp], p2[main:rp]]
            if u is not None:
                parts += list(split(u))
            rhs = jnp.concatenate(parts, axis=0)
            return fold(dot32(w_ref[e, :, 0:rhs.shape[0]], rhs))

        def couple(e, u):
            return fold(dot32(n_ref[e], jnp.concatenate(list(split(u)), axis=0)))

        def step(i, carry):
            es = [units[i + s * trips] for s in range(STREAMS)]
            y0 = [y[e] for e in es]
            p = [rates(v, e) for v, e in zip(y0, es)]
            g1 = [section(a, e) for a, e in zip(p, es)]
            p = [rates(v + 2.0 * g, e) for v, g, e in zip(y0, g1, es)]
            g2 = [section(a, e, -8.0 * g) for a, g, e in zip(p, g1, es)]
            p = [rates(v + 1.92 * a + 0.24 * b, e) for v, a, b, e in zip(y0, g1, g2, es)]
            g3 = [section(q, e, 14.88 * a + 2.4 * b) for q, a, b, e in zip(p, g1, g2, es)]
            g4 = [
                c + couple(e, -15.776 * a - 2.832 * b - 0.4 * c)
                for a, b, c, e in zip(g1, g2, g3, es)
            ]
            for v, a, b, c, d, e in zip(y0, g1, g2, g3, g4, es):
                y[e] = (
                    v + (19.0 / 9.0) * a + 0.5 * b + (25.0 / 108.0) * c + (125.0 / 108.0) * d
                )
            return carry

        lax.fori_loop(0, trips, step, 0)

        big_out.wait()
        for e in range(listed):
            @pl.when(reacts(e))
            def _():
                ybuf[e] = y[e, 0:species, :]
                deliver(e).start()
        for e in range(listed):
            @pl.when(reacts(e))
            def _():
                deliver(e).wait()

    scratch = [
        pltpu.VMEM((species, blocks, cells), F32),
        pltpu.VMEM((listed, species, cells), F32),
        pltpu.VMEM((listed + 1, sp, cells), F32),
        pltpu.VMEM((listed + 1, rp, cells), F32),
        pltpu.VMEM((listed + 1, 2 * sp, wide), BF16),
        pltpu.VMEM((listed + 1, 2 * sp, 2 * sp), BF16),
        pltpu.VMEM((2 * rp, 4 * sp), BF16),
        pltpu.VMEM((sp, wide), F32),
        pltpu.VMEM((2, rp, cells), F32),
        pltpu.VMEM((sp, up(reactions, 128)), F32),
        pltpu.SMEM((STREAMS * listed * SUBS + STREAMS * SUBS,), jnp.int32),
        pltpu.VMEM((blocks, cells), F32),
        pltpu.SMEM((blocks,), jnp.int32),
        pltpu.SMEM((listed,), jnp.int32),
        pltpu.SMEM((listed,), jnp.int32),
        pltpu.VMEM((listed, species, species), F32),
        pltpu.VMEM((reactions,), F32),
        pltpu.VMEM((reactions,), F32),
        pltpu.VMEM((species, reactions), F32),
        pltpu.VMEM((species, reactions), F32),
        pltpu.VMEM((species, reactions), F32),
        pltpu.SemaphoreType.DMA,
        pltpu.SemaphoreType.DMA,
        pltpu.SemaphoreType.DMA((listed,)),
        pltpu.SemaphoreType.DMA((10,)),
    ]
    return kernel, scratch


def on_device(
    composition,
    heat_level,
    step_counts,
    burning_parcel_roster,
    target_compute_place,
    partial_reciprocal_operator,
    speed_log_prefactor,
    arrhenius_barrier,
    leading_ingredient,
    trailing_ingredient,
    molar_coefficients,
):
    blocks, species, cells = composition.shape
    reactions = speed_log_prefactor.shape[0]
    listed = burning_parcel_roster.shape[0]
    kernel, scratch = make_kernel(species, reactions, blocks, cells, listed)
    hbm = pl.BlockSpec(memory_space=pltpu.HBM)
    out = pl.pallas_call(
        kernel,
        out_shape=jax.ShapeDtypeStruct((species, blocks, cells), composition.dtype),
        in_specs=[hbm] * 11,
        out_specs=hbm,
        scratch_shapes=scratch,
        compiler_params=pltpu.CompilerParams(vmem_limit_bytes=67043328),
        name="integrate",
    )(
        jnp.transpose(composition, (1, 0, 2)),
        heat_level,
        step_counts,
        burning_parcel_roster,
        target_compute_place,
        partial_reciprocal_operator,
        speed_log_prefactor,
        arrhenius_barrier,
        leading_ingredient.T,
        trailing_ingredient.T,
        molar_coefficients,
    )
    return jnp.transpose(out, (1, 0, 2))


def solution(mesh):
    owners = tuple(mesh.axis_names)
    return jax.shard_map(
        on_device,
        mesh=mesh,
        in_specs=(
            P(owners, None, None),
            P(owners, None),
            P(owners),
            P(owners),
            P(owners),
            P(owners, None, None),
            P(),
            P(),
            P(),
            P(),
            P(),
        ),
        out_specs=P(owners, None, None),
        check_vma=False,
    )
```

```python
import jax
import jax.numpy as jnp
from jax import lax
from jax.experimental import pallas as pl
from jax.experimental.pallas import tpu as pltpu
from jax.sharding import PartitionSpec as P

SUBS = 3
STREAMS = 4
LOG2E = 1.4426950408889634

F32 = jnp.float32
BF16 = jnp.bfloat16


def up(n, m):
    return (n + m - 1) // m * m


def dot32(a, b):
    return jnp.dot(a, b, preferred_element_type=F32)


def split(v):
    hi = v.astype(BF16)
    return hi, (v - hi.astype(F32)).astype(BF16)


def make_kernel(species, reactions, blocks, cells, listed):
    sp = up(species, 64)
    sr = up(species, 8)
    rp = up(reactions, 16)
    main = reactions // 128 * 128
    tail = rp - main
    at_g = main
    at_t = main + 2 * sp
    wide = at_t + 128
    padded = up(reactions, 128)

    def kernel(
        comp, heat_at, counts_at, roster_at, target_at, inverse_at, pref_at, barr_at, lead_at,
        trail_at, molar_at,
        out,
        bulk, ybuf, y, kf, w_ref, a_ref, minv, cols, stage, units,
        heat, counts, roster, target, inverse, pref, barr, lead, trail, molar,
        sem_in, sem_out, sem_y, sem_a,
    ):
        loads = [
            pltpu.make_async_copy(src, dst, sem_a.at[i])
            for i, (src, dst) in enumerate((
                (roster_at, roster), (target_at, target), (counts_at, counts),
                (lead_at, lead), (trail_at, trail), (pref_at, pref), (barr_at, barr),
                (molar_at, molar), (heat_at, heat), (inverse_at, inverse),
            ))
        ]
        for load in loads:
            load.start()
        big_in = pltpu.make_async_copy(comp, bulk, sem_in)
        big_out = pltpu.make_async_copy(bulk, out, sem_out)

        def reacts(e):
            return target[e] >= 0

        def fetch(e):
            return pltpu.make_async_copy(comp.at[:, roster[e], :], ybuf.at[e], sem_y.at[e])

        def deliver(e):
            return pltpu.make_async_copy(ybuf.at[e], out.at[:, roster[e], :], sem_y.at[e])

        y[...] = jnp.zeros(y.shape, F32)
        kf[listed] = jnp.zeros((rp, cells), F32)
        w_ref[listed] = jnp.zeros((2 * sr, wide), BF16)
        minv[...] = jnp.zeros(minv.shape, F32)
        stage[...] = jnp.zeros(stage.shape, F32)

        for load in loads[:3]:
            load.wait()
        for e in range(listed):
            fetch(e).start()
        big_in.start()

        total = jnp.int32(0)
        longest = jnp.int32(0)
        for i in range(units.shape[0]):
            units[i] = listed
        for e in range(listed):
            w = jnp.where(reacts(e), counts[roster[e]], 0)
            for k in range(SUBS):
                @pl.when(k < w)
                def _(total=total, k=k, e=e):
                    units[total + k] = e
            total = total + w
            longest = jnp.maximum(longest, w)
        trips = jnp.maximum((total + STREAMS - 1) // STREAMS, longest)

        for load in loads[3:]:
            load.wait()
        stage[0, 0:species, 0:reactions] = lead[...]
        stage[1, 0:species, 0:reactions] = trail[...]
        stage[2, 0:species, 0:reactions] = molar[...]
        stage[3, 0:1, 0:reactions] = pref[...].reshape(1, reactions) * LOG2E
        stage[3, 1:2, 0:reactions] = barr[...].reshape(1, reactions) * LOG2E
        for i in range(2):
            full = stage[i]
            hi = full.astype(BF16).astype(F32)
            turned = jnp.concatenate([hi, full - hi], axis=0).T[0:rp].astype(BF16)
            a_ref[i * rp:(i + 1) * rp, 0:2 * sp] = turned
            a_ref[i * rp:(i + 1) * rp, 2 * sp:3 * sp] = turned[:, 0:sp]
        turned = stage[3, 0:8, :].T
        cols[0] = jnp.broadcast_to(turned[0:rp, 0:1], (rp, cells))
        cols[1] = jnp.broadcast_to(turned[0:rp, 1:2], (rp, cells))

        row = lax.broadcasted_iota(jnp.int32, (sp, 2 * sp), 0)
        col = lax.broadcasted_iota(jnp.int32, (sp, 2 * sp), 1)
        eye = jnp.where((col == row) | (col == row + sp), 5.0, 0.0).astype(F32)
        rest = stage[2, :, main:main + 128]
        rest = rest + pltpu.roll(rest, tail, 1)
        call = jnp.concatenate([stage[2, :, 0:main], eye, rest], axis=1)
        c1, c2 = split(call)
        for e in range(listed):
            minv[e * sr:e * sr + species, 0:species] = inverse[e]
        whole = minv[...]
        hi = whole.astype(BF16).astype(F32)
        lo = pltpu.roll(whole - hi, sp, 1)
        lhs = jnp.concatenate([(hi + lo).astype(BF16), hi.astype(BF16)[:, 0:sp]], axis=1)
        ops = dot32(lhs, jnp.concatenate([c1, c1, c2], axis=0))
        lane = lax.broadcasted_iota(jnp.int32, (1, wide), 1)
        coupled = (lane >= at_g) & (lane < at_t)
        for e in range(listed):
            weight = counts[roster[e]].astype(F32)
            scaled = ops[e * sr:(e + 1) * sr]
            scaled = scaled * jnp.where(coupled, 1.0, 1.0 / weight)
            hi = scaled.astype(BF16).astype(F32)
            w_ref[e] = jnp.concatenate([hi, scaled - hi], axis=0).astype(BF16)

        big_in.wait()
        big_out.start()

        def prepare(e, carry):
            warm = 1000.0 / heat[pl.ds(roster[e], 1), :] - 0.6
            kf[e] = jnp.exp2(cols[0] - cols[1] * warm)
            fetch(e).wait()
            y[e, 0:species, :] = ybuf[e]
            return carry

        lax.fori_loop(0, listed, prepare, 0)

        def parts_of(v):
            return split(jnp.concatenate([v, jnp.zeros((sp - sr, cells), F32)], axis=0))

        def rates(v, e):
            x1, x2 = parts_of(v)
            z = dot32(a_ref[...], jnp.concatenate([x1, x1, x2], axis=0))
            return split(kf[e] * z[0:rp] * z[rp:2 * rp])

        def fold(o):
            return o[0:sr] + o[sr:2 * sr]

        def section(p, e, u=None):
            p1, p2 = p
            ends = [p1[main:rp], p2[main:rp]]
            if u is None:
                lhs = jnp.concatenate(
                    [w_ref[e, :, 0:main], w_ref[e, :, at_t:at_t + 2 * tail]], axis=1
                )
            else:
                ends = list(parts_of(u)) + ends
                lhs = w_ref[e, :, 0:at_t + 2 * tail]
            o = fold(dot32(lhs, jnp.concatenate([p1[0:main]] + ends, axis=0)))
            return o + dot32(w_ref[e, 0:sp, 0:main], p2[0:main])[0:sr]

        def couple(e, u):
            return fold(dot32(w_ref[e, :, at_g:at_t], jnp.concatenate(list(parts_of(u)), axis=0)))

        def step(i, carry):
            es = [units[i + s * trips] for s in range(STREAMS)]
            y0 = [y[e] for e in es]
            p = [rates(v, e) for v, e in zip(y0, es)]
            g1 = [section(a, e) for a, e in zip(p, es)]
            p = [rates(v + 2.0 * g, e) for v, g, e in zip(y0, g1, es)]
            g2 = [section(a, e, -8.0 * g) for a, g, e in zip(p, g1, es)]
            p = [rates(v + 1.92 * a + 0.24 * b, e) for v, a, b, e in zip(y0, g1, g2, es)]
            g3 = [section(q, e, 14.88 * a + 2.4 * b) for q, a, b, e in zip(p, g1, g2, es)]
            g4 = [
                c + couple(e, -15.776 * a - 2.832 * b - 0.4 * c)
                for a, b, c, e in zip(g1, g2, g3, es)
            ]
            for v, a, b, c, d, e in zip(y0, g1, g2, g3, g4, es):
                y[e] = (
                    v + (19.0 / 9.0) * a + 0.5 * b + (25.0 / 108.0) * c + (125.0 / 108.0) * d
                )
            return carry

        lax.fori_loop(0, trips, step, 0)

        big_out.wait()
        for e in range(listed):
            @pl.when(reacts(e))
            def _():
                ybuf[e] = y[e, 0:species, :]
                deliver(e).start()
        for e in range(listed):
            @pl.when(reacts(e))
            def _():
                deliver(e).wait()

    scratch = [
        pltpu.VMEM((species, blocks, cells), F32),
        pltpu.VMEM((listed, species, cells), F32),
        pltpu.VMEM((listed + 1, sr, cells), F32),
        pltpu.VMEM((listed + 1, rp, cells), F32),
        pltpu.VMEM((listed + 1, 2 * sr, wide), BF16),
        pltpu.VMEM((2 * rp, 3 * sp), BF16),
        pltpu.VMEM((listed * sr, 128), F32),
        pltpu.VMEM((2, rp, cells), F32),
        pltpu.VMEM((4, sp, padded), F32),
        pltpu.SMEM((listed * SUBS + STREAMS * SUBS,), jnp.int32),
        pltpu.VMEM((blocks, cells), F32),
        pltpu.SMEM((blocks,), jnp.int32),
        pltpu.SMEM((listed,), jnp.int32),
        pltpu.SMEM((listed,), jnp.int32),
        pltpu.VMEM((listed, species, species), F32),
        pltpu.VMEM((reactions,), F32),
        pltpu.VMEM((reactions,), F32),
        pltpu.VMEM((species, reactions), F32),
        pltpu.VMEM((species, reactions), F32),
        pltpu.VMEM((species, reactions), F32),
        pltpu.SemaphoreType.DMA,
        pltpu.SemaphoreType.DMA,
        pltpu.SemaphoreType.DMA((listed,)),
        pltpu.SemaphoreType.DMA((10,)),
    ]
    return kernel, scratch


def on_device(
    composition,
    heat_level,
    step_counts,
    burning_parcel_roster,
    target_compute_place,
    partial_reciprocal_operator,
    speed_log_prefactor,
    arrhenius_barrier,
    leading_ingredient,
    trailing_ingredient,
    molar_coefficients,
):
    blocks, species, cells = composition.shape
    reactions = speed_log_prefactor.shape[0]
    listed = burning_parcel_roster.shape[0]
    kernel, scratch = make_kernel(species, reactions, blocks, cells, listed)
    hbm = pl.BlockSpec(memory_space=pltpu.HBM)
    out = pl.pallas_call(
        kernel,
        out_shape=jax.ShapeDtypeStruct((species, blocks, cells), composition.dtype),
        in_specs=[hbm] * 11,
        out_specs=hbm,
        scratch_shapes=scratch,
        compiler_params=pltpu.CompilerParams(vmem_limit_bytes=67043328),
        name="integrate",
    )(
        jnp.transpose(composition, (1, 0, 2)),
        heat_level,
        step_counts,
        burning_parcel_roster,
        target_compute_place,
        partial_reciprocal_operator,
        speed_log_prefactor,
        arrhenius_barrier,
        leading_ingredient.T,
        trailing_ingredient.T,
        molar_coefficients,
    )
    return jnp.transpose(out, (1, 0, 2))


def solution(mesh):
    owners = tuple(mesh.axis_names)
    return jax.shard_map(
        on_device,
        mesh=mesh,
        in_specs=(
            P(owners, None, None),
            P(owners, None),
            P(owners),
            P(owners),
            P(owners),
            P(owners, None, None),
            P(),
            P(),
            P(),
            P(),
            P(),
        ),
        out_specs=P(owners, None, None),
        check_vma=False,
    )
```

```python
import jax
import jax.numpy as jnp
from jax import lax
from jax.experimental import pallas as pl
from jax.experimental.pallas import tpu as pltpu
from jax.sharding import PartitionSpec as P

SUBS = 3
STREAMS = 4
LOG2E = 1.4426950408889634

F32 = jnp.float32
BF16 = jnp.bfloat16


def up(n, m):
    return (n + m - 1) // m * m


def dot32(a, b):
    return jnp.dot(a, b, preferred_element_type=F32)


def split(v):
    hi = v.astype(BF16)
    return hi, (v - hi.astype(F32)).astype(BF16)


def make_kernel(species, reactions, blocks, cells, listed):
    sp = up(species, 64)
    sr = up(species, 8)
    rp = up(reactions, 16)
    main = reactions // 128 * 128
    tail = rp - main
    at_g = main
    at_t = main + 2 * sp
    wide = at_t + 128
    padded = up(reactions, 128)
    rounds = max((listed * SUBS + STREAMS - 1) // STREAMS, SUBS)

    def kernel(
        comp, heat_at, counts_at, roster_at, target_at, inverse_at, pref_at, barr_at, lead_at,
        trail_at, molar_at,
        out,
        bulk, ybuf, y, kf, w_ref, a_ref, minv, cols, stage, units,
        heat, counts, roster, target, inverse, pref, barr, lead, trail, molar,
        sem_in, sem_out, sem_y, sem_a,
    ):
        loads = [
            pltpu.make_async_copy(src, dst, sem_a.at[i])
            for i, (src, dst) in enumerate((
                (roster_at, roster), (target_at, target), (counts_at, counts),
                (lead_at, lead), (trail_at, trail), (pref_at, pref), (barr_at, barr),
                (molar_at, molar), (heat_at, heat), (inverse_at, inverse),
            ))
        ]
        for load in loads:
            load.start()
        big_in = pltpu.make_async_copy(comp, bulk, sem_in)
        big_out = pltpu.make_async_copy(bulk, out, sem_out)

        def reacts(e):
            return target[e] >= 0

        def fetch(e):
            return pltpu.make_async_copy(comp.at[:, roster[e], :], ybuf.at[e], sem_y.at[e])

        def deliver(e):
            return pltpu.make_async_copy(ybuf.at[e], out.at[:, roster[e], :], sem_y.at[e])

        y[...] = jnp.zeros(y.shape, F32)
        kf[listed] = jnp.zeros((rp, cells), F32)
        w_ref[listed] = jnp.zeros((2 * sr, wide), BF16)
        minv[...] = jnp.zeros(minv.shape, F32)
        stage[...] = jnp.zeros(stage.shape, F32)

        for load in loads[:3]:
            load.wait()
        for e in range(listed):
            fetch(e).start()
        big_in.start()

        left = [jnp.where(reacts(e), counts[roster[e]], 0) for e in range(listed)]
        trips = jnp.int32(0)
        fours = jnp.int32(0)
        for r in range(rounds):
            keys = [jnp.where(n > 0, n * 64 + e, -1) for e, n in enumerate(left)]
            for s in range(STREAMS):
                top = keys[0]
                for key in keys[1:]:
                    top = jnp.maximum(top, key)
                found = top >= 0
                units[r * STREAMS + s] = jnp.where(found, top & 63, listed)
                if s == 0:
                    trips = trips + found.astype(jnp.int32)
                if s == STREAMS // 2:
                    fours = fours + found.astype(jnp.int32)
                for e in range(listed):
                    hit = found & (keys[e] == top)
                    left[e] = jnp.where(hit, left[e] - 1, left[e])
                    keys[e] = jnp.where(hit, -1, keys[e])

        for load in loads[3:]:
            load.wait()
        stage[0, 0:species, 0:reactions] = lead[...]
        stage[1, 0:species, 0:reactions] = trail[...]
        stage[2, 0:species, 0:reactions] = molar[...]
        stage[3, 0:1, 0:reactions] = pref[...].reshape(1, reactions) * LOG2E
        stage[3, 1:2, 0:reactions] = barr[...].reshape(1, reactions) * LOG2E
        for i in range(2):
            full = stage[i]
            hi = full.astype(BF16).astype(F32)
            turned = jnp.concatenate([hi, full - hi], axis=0).T[0:rp].astype(BF16)
            a_ref[i * rp:(i + 1) * rp, 0:2 * sp] = turned
            a_ref[i * rp:(i + 1) * rp, 2 * sp:3 * sp] = turned[:, 0:sp]
        turned = stage[3, 0:8, :].T
        cols[0] = jnp.broadcast_to(turned[0:rp, 0:1], (rp, cells))
        cols[1] = jnp.broadcast_to(turned[0:rp, 1:2], (rp, cells))

        row = lax.broadcasted_iota(jnp.int32, (sp, 2 * sp), 0)
        col = lax.broadcasted_iota(jnp.int32, (sp, 2 * sp), 1)
        eye = jnp.where((col == row) | (col == row + sp), 5.0, 0.0).astype(F32)
        rest = stage[2, :, main:main + 128]
        rest = rest + pltpu.roll(rest, tail, 1)
        call = jnp.concatenate([stage[2, :, 0:main], eye, rest], axis=1)
        c1, c2 = split(call)
        for e in range(listed):
            minv[e * sr:e * sr + species, 0:species] = inverse[e]
        whole = minv[...]
        hi = whole.astype(BF16).astype(F32)
        lo = pltpu.roll(whole - hi, sp, 1)
        lhs = jnp.concatenate([(hi + lo).astype(BF16), hi.astype(BF16)[:, 0:sp]], axis=1)
        ops = dot32(lhs, jnp.concatenate([c1, c1, c2], axis=0))
        lane = lax.broadcasted_iota(jnp.int32, (1, wide), 1)
        coupled = (lane >= at_g) & (lane < at_t)
        for e in range(listed):
            weight = counts[roster[e]].astype(F32)
            scaled = ops[e * sr:(e + 1) * sr]
            scaled = scaled * jnp.where(coupled, 1.0, 1.0 / weight)
            hi = scaled.astype(BF16).astype(F32)
            w_ref[e] = jnp.concatenate([hi, scaled - hi], axis=0).astype(BF16)

        def prepare(e, carry):
            warm = 1000.0 / heat[pl.ds(roster[e], 1), :] - 0.6
            kf[e] = jnp.exp2(cols[0] - cols[1] * warm)
            fetch(e).wait()
            y[e, 0:species, :] = ybuf[e]
            return carry

        lax.fori_loop(0, listed, prepare, 0)

        def parts_of(v):
            return split(jnp.concatenate([v, jnp.zeros((sp - sr, cells), F32)], axis=0))

        def rates(v, e):
            x1, x2 = parts_of(v)
            z = dot32(a_ref[...], jnp.concatenate([x1, x1, x2], axis=0))
            return split(kf[e] * z[0:rp] * z[rp:2 * rp])

        def fold(o):
            return o[0:sr] + o[sr:2 * sr]

        def section(p, e, u=None):
            p1, p2 = p
            ends = [p1[main:rp], p2[main:rp]]
            if u is None:
                lhs = jnp.concatenate(
                    [w_ref[e, :, 0:main], w_ref[e, :, at_t:at_t + 2 * tail]], axis=1
                )
            else:
                ends = list(parts_of(u)) + ends
                lhs = w_ref[e, :, 0:at_t + 2 * tail]
            o = fold(dot32(lhs, jnp.concatenate([p1[0:main]] + ends, axis=0)))
            return o + dot32(w_ref[e, 0:sp, 0:main], p2[0:main])[0:sr]

        def couple(e, u):
            return fold(dot32(w_ref[e, :, at_g:at_t], jnp.concatenate(list(parts_of(u)), axis=0)))

        def turn_round():
            big_in.wait()
            big_out.start()

        def advance(i, width):
            es = [units[i * STREAMS + s] for s in range(width)]
            y0 = [y[e] for e in es]
            p = [rates(v, e) for v, e in zip(y0, es)]
            g1 = [section(a, e) for a, e in zip(p, es)]
            p = [rates(v + 2.0 * g, e) for v, g, e in zip(y0, g1, es)]
            g2 = [section(a, e, -8.0 * g) for a, g, e in zip(p, g1, es)]
            p = [rates(v + 1.92 * a + 0.24 * b, e) for v, a, b, e in zip(y0, g1, g2, es)]
            g3 = [section(q, e, 14.88 * a + 2.4 * b) for q, a, b, e in zip(p, g1, g2, es)]
            g4 = [
                c + couple(e, -15.776 * a - 2.832 * b - 0.4 * c)
                for a, b, c, e in zip(g1, g2, g3, es)
            ]
            for v, a, b, c, d, e in zip(y0, g1, g2, g3, g4, es):
                y[e] = (
                    v + (19.0 / 9.0) * a + 0.5 * b + (25.0 / 108.0) * c + (125.0 / 108.0) * d
                )

        def full_step(i, carry):
            advance(i, STREAMS)

            @pl.when(i == 0)
            def _():
                turn_round()

            return carry

        def half_step(i, carry):
            advance(i, STREAMS // 2)
            return carry

        lax.fori_loop(0, fours, full_step, 0)

        @pl.when(fours == 0)
        def _():
            turn_round()

        lax.fori_loop(fours, trips, half_step, 0)

        big_out.wait()
        for e in range(listed):
            @pl.when(reacts(e))
            def _():
                ybuf[e] = y[e, 0:species, :]
                deliver(e).start()
        for e in range(listed):
            @pl.when(reacts(e))
            def _():
                deliver(e).wait()

    scratch = [
        pltpu.VMEM((species, blocks, cells), F32),
        pltpu.VMEM((listed, species, cells), F32),
        pltpu.VMEM((listed + 1, sr, cells), F32),
        pltpu.VMEM((listed + 1, rp, cells), F32),
        pltpu.VMEM((listed + 1, 2 * sr, wide), BF16),
        pltpu.VMEM((2 * rp, 3 * sp), BF16),
        pltpu.VMEM((listed * sr, 128), F32),
        pltpu.VMEM((2, rp, cells), F32),
        pltpu.VMEM((4, sp, padded), F32),
        pltpu.SMEM((rounds * STREAMS,), jnp.int32),
        pltpu.VMEM((blocks, cells), F32),
        pltpu.SMEM((blocks,), jnp.int32),
        pltpu.SMEM((listed,), jnp.int32),
        pltpu.SMEM((listed,), jnp.int32),
        pltpu.VMEM((listed, species, species), F32),
        pltpu.VMEM((reactions,), F32),
        pltpu.VMEM((reactions,), F32),
        pltpu.VMEM((species, reactions), F32),
        pltpu.VMEM((species, reactions), F32),
        pltpu.VMEM((species, reactions), F32),
        pltpu.SemaphoreType.DMA,
        pltpu.SemaphoreType.DMA,
        pltpu.SemaphoreType.DMA((listed,)),
        pltpu.SemaphoreType.DMA((10,)),
    ]
    return kernel, scratch


def on_device(
    composition,
    heat_level,
    step_counts,
    burning_parcel_roster,
    target_compute_place,
    partial_reciprocal_operator,
    speed_log_prefactor,
    arrhenius_barrier,
    leading_ingredient,
    trailing_ingredient,
    molar_coefficients,
):
    blocks, species, cells = composition.shape
    reactions = speed_log_prefactor.shape[0]
    listed = burning_parcel_roster.shape[0]
    kernel, scratch = make_kernel(species, reactions, blocks, cells, listed)
    hbm = pl.BlockSpec(memory_space=pltpu.HBM)
    out = pl.pallas_call(
        kernel,
        out_shape=jax.ShapeDtypeStruct((species, blocks, cells), composition.dtype),
        in_specs=[hbm] * 11,
        out_specs=hbm,
        scratch_shapes=scratch,
        compiler_params=pltpu.CompilerParams(vmem_limit_bytes=67043328),
        name="integrate",
    )(
        jnp.transpose(composition, (1, 0, 2)),
        heat_level,
        step_counts,
        burning_parcel_roster,
        target_compute_place,
        partial_reciprocal_operator,
        speed_log_prefactor,
        arrhenius_barrier,
        leading_ingredient.T,
        trailing_ingredient.T,
        molar_coefficients,
    )
    return jnp.transpose(out, (1, 0, 2))


def solution(mesh):
    owners = tuple(mesh.axis_names)
    return jax.shard_map(
        on_device,
        mesh=mesh,
        in_specs=(
            P(owners, None, None),
            P(owners, None),
            P(owners),
            P(owners),
            P(owners),
            P(owners, None, None),
            P(),
            P(),
            P(),
            P(),
            P(),
        ),
        out_specs=P(owners, None, None),
        check_vma=False,
    )
```

```python
import jax
import jax.numpy as jnp
from jax import lax
from jax.experimental import pallas as pl
from jax.experimental.pallas import tpu as pltpu
from jax.sharding import PartitionSpec as P

SUBS = 3
STREAMS = 4
LOG2E = 1.4426950408889634

F32 = jnp.float32
BF16 = jnp.bfloat16


def up(n, m):
    return (n + m - 1) // m * m


def dot32(a, b):
    return jnp.dot(a, b, preferred_element_type=F32)


def split(v):
    hi = v.astype(BF16)
    return hi, (v - hi.astype(F32)).astype(BF16)


def make_kernel(species, reactions, blocks, cells, listed):
    sp = up(species, 64)
    sr = up(species, 8)
    rp = up(reactions, 16)
    main = reactions // 128 * 128
    tail = rp - main
    at_g = main
    at_t = main + 2 * sp
    wide = at_t + 128
    padded = up(reactions, 128)
    rounds = max((listed * SUBS + STREAMS - 1) // STREAMS, SUBS)

    def kernel(
        comp, heat_at, counts_at, roster_at, target_at, inverse_at, pref_at, barr_at, lead_at,
        trail_at, molar_at,
        out,
        bulk, ybuf, y, kf, w_ref, a_ref, minv, cols, stage, units,
        heat, counts, roster, target, inverse, pref, barr, lead, trail, molar,
        sem_in, sem_out, sem_y, sem_a,
    ):
        loads = [
            pltpu.make_async_copy(src, dst, sem_a.at[i])
            for i, (src, dst) in enumerate((
                (roster_at, roster), (target_at, target), (counts_at, counts),
                (lead_at, lead), (trail_at, trail), (pref_at, pref), (barr_at, barr),
                (molar_at, molar), (heat_at, heat), (inverse_at, inverse),
            ))
        ]
        for load in loads:
            load.start()
        big_in = pltpu.make_async_copy(comp, bulk, sem_in)
        big_out = pltpu.make_async_copy(bulk, out, sem_out)

        def reacts(e):
            return target[e] >= 0

        def fetch(e):
            return pltpu.make_async_copy(comp.at[:, roster[e], :], ybuf.at[e], sem_y.at[e])

        def deliver(e):
            return pltpu.make_async_copy(ybuf.at[e], out.at[:, roster[e], :], sem_y.at[e])

        y[...] = jnp.zeros(y.shape, F32)
        kf[listed] = jnp.zeros((rp, cells), F32)
        w_ref[listed] = jnp.zeros((2 * sr, wide), BF16)
        minv[...] = jnp.zeros(minv.shape, F32)
        stage[...] = jnp.zeros(stage.shape, F32)

        for load in loads[:3]:
            load.wait()
        for e in range(listed):
            fetch(e).start()
        big_in.start()

        for load in loads[3:]:
            load.wait()

        left = [jnp.where(reacts(e), counts[roster[e]], 0) for e in range(listed)]
        trips = jnp.int32(0)
        fours = jnp.int32(0)
        for r in range(rounds):
            keys = [jnp.where(n > 0, n * 64 + e, -1) for e, n in enumerate(left)]
            for s in range(STREAMS):
                top = keys[0]
                for key in keys[1:]:
                    top = jnp.maximum(top, key)
                found = top >= 0
                units[r * STREAMS + s] = jnp.where(found, top & 63, listed)
                if s == 0:
                    trips = trips + found.astype(jnp.int32)
                if s == STREAMS // 2:
                    fours = fours + found.astype(jnp.int32)
                for e in range(listed):
                    hit = found & (keys[e] == top)
                    left[e] = jnp.where(hit, left[e] - 1, left[e])
                    keys[e] = jnp.where(hit, -1, keys[e])

        stage[0, 0:species, 0:reactions] = lead[...]
        stage[1, 0:species, 0:reactions] = trail[...]
        stage[2, 0:species, 0:reactions] = molar[...]
        stage[3, 0:1, 0:reactions] = pref[...].reshape(1, reactions) * LOG2E
        stage[3, 1:2, 0:reactions] = barr[...].reshape(1, reactions) * LOG2E
        for i in range(2):
            full = stage[i]
            hi = full.astype(BF16).astype(F32)
            turned = jnp.concatenate([hi, full - hi], axis=0).T[0:rp].astype(BF16)
            a_ref[i * rp:(i + 1) * rp, 0:2 * sp] = turned
            a_ref[i * rp:(i + 1) * rp, 2 * sp:3 * sp] = turned[:, 0:sp]
        turned = stage[3, 0:8, :].T
        cols[0] = jnp.broadcast_to(turned[0:rp, 0:1], (rp, cells))
        cols[1] = jnp.broadcast_to(turned[0:rp, 1:2], (rp, cells))

        row = lax.broadcasted_iota(jnp.int32, (sp, 2 * sp), 0)
        col = lax.broadcasted_iota(jnp.int32, (sp, 2 * sp), 1)
        eye = jnp.where((col == row) | (col == row + sp), 5.0, 0.0).astype(F32)
        rest = stage[2, :, main:main + 128]
        rest = rest + pltpu.roll(rest, tail, 1)
        call = jnp.concatenate([stage[2, :, 0:main], eye, rest], axis=1)
        c1, c2 = split(call)
        for e in range(listed):
            minv[e * sr:e * sr + species, 0:species] = inverse[e]
        whole = minv[...]
        hi = whole.astype(BF16).astype(F32)
        lo = pltpu.roll(whole - hi, sp, 1)
        lhs = jnp.concatenate([(hi + lo).astype(BF16), hi.astype(BF16)[:, 0:sp]], axis=1)
        ops = dot32(lhs, jnp.concatenate([c1, c1, c2], axis=0))
        lane = lax.broadcasted_iota(jnp.int32, (1, wide), 1)
        coupled = (lane >= at_g) & (lane < at_t)
        for e in range(listed):
            weight = counts[roster[e]].astype(F32)
            scaled = ops[e * sr:(e + 1) * sr]
            scaled = scaled * jnp.where(coupled, 1.0, 1.0 / weight)
            hi = scaled.astype(BF16).astype(F32)
            w_ref[e] = jnp.concatenate([hi, scaled - hi], axis=0).astype(BF16)

        for e in range(listed):
            warm = 1000.0 / heat[pl.ds(roster[e], 1), :] - 0.6
            kf[e] = jnp.exp2(cols[0] - cols[1] * warm)
        for e in range(listed):
            fetch(e).wait()
        for e in range(listed):
            y[e, 0:species, :] = ybuf[e]

        def parts_of(v):
            return split(jnp.concatenate([v, jnp.zeros((sp - sr, cells), F32)], axis=0))

        def rates(v, e):
            x1, x2 = parts_of(v)
            z = dot32(a_ref[...], jnp.concatenate([x1, x1, x2], axis=0))
            return split(kf[e] * z[0:rp] * z[rp:2 * rp])

        def fold(o):
            return o[0:sr] + o[sr:2 * sr]

        def section(p, e, u=None):
            p1, p2 = p
            ends = [p1[main:rp], p2[main:rp]]
            if u is None:
                lhs = jnp.concatenate(
                    [w_ref[e, :, 0:main], w_ref[e, :, at_t:at_t + 2 * tail]], axis=1
                )
            else:
                ends = list(parts_of(u)) + ends
                lhs = w_ref[e, :, 0:at_t + 2 * tail]
            o = fold(dot32(lhs, jnp.concatenate([p1[0:main]] + ends, axis=0)))
            return o + dot32(w_ref[e, 0:sp, 0:main], p2[0:main])[0:sr]

        def couple(e, u):
            return fold(dot32(w_ref[e, :, at_g:at_t], jnp.concatenate(list(parts_of(u)), axis=0)))

        def turn_round():
            big_in.wait()
            big_out.start()

        def advance(i, width):
            es = [units[i * STREAMS + s] for s in range(width)]
            y0 = [y[e] for e in es]
            p = [rates(v, e) for v, e in zip(y0, es)]
            g1 = [section(a, e) for a, e in zip(p, es)]
            p = [rates(v + 2.0 * g, e) for v, g, e in zip(y0, g1, es)]
            g2 = [section(a, e, -8.0 * g) for a, g, e in zip(p, g1, es)]
            p = [rates(v + 1.92 * a + 0.24 * b, e) for v, a, b, e in zip(y0, g1, g2, es)]
            g3 = [section(q, e, 14.88 * a + 2.4 * b) for q, a, b, e in zip(p, g1, g2, es)]
            g4 = [
                c + couple(e, -15.776 * a - 2.832 * b - 0.4 * c)
                for a, b, c, e in zip(g1, g2, g3, es)
            ]
            for v, a, b, c, d, e in zip(y0, g1, g2, g3, g4, es):
                y[e] = (
                    v + (19.0 / 9.0) * a + 0.5 * b + (25.0 / 108.0) * c + (125.0 / 108.0) * d
                )

        def full_step(i, carry):
            advance(i, STREAMS)

            @pl.when(i == 0)
            def _():
                turn_round()

            return carry

        def half_step(i, carry):
            advance(i, STREAMS // 2)
            return carry

        lax.fori_loop(0, fours, full_step, 0)

        @pl.when(fours == 0)
        def _():
            turn_round()

        lax.fori_loop(fours, trips, half_step, 0)

        big_out.wait()
        for e in range(listed):
            @pl.when(reacts(e))
            def _():
                ybuf[e] = y[e, 0:species, :]
                deliver(e).start()
        for e in range(listed):
            @pl.when(reacts(e))
            def _():
                deliver(e).wait()

    scratch = [
        pltpu.VMEM((species, blocks, cells), F32),
        pltpu.VMEM((listed, species, cells), F32),
        pltpu.VMEM((listed + 1, sr, cells), F32),
        pltpu.VMEM((listed + 1, rp, cells), F32),
        pltpu.VMEM((listed + 1, 2 * sr, wide), BF16),
        pltpu.VMEM((2 * rp, 3 * sp), BF16),
        pltpu.VMEM((listed * sr, 128), F32),
        pltpu.VMEM((2, rp, cells), F32),
        pltpu.VMEM((4, sp, padded), F32),
        pltpu.SMEM((rounds * STREAMS,), jnp.int32),
        pltpu.VMEM((blocks, cells), F32),
        pltpu.SMEM((blocks,), jnp.int32),
        pltpu.SMEM((listed,), jnp.int32),
        pltpu.SMEM((listed,), jnp.int32),
        pltpu.VMEM((listed, species, species), F32),
        pltpu.VMEM((reactions,), F32),
        pltpu.VMEM((reactions,), F32),
        pltpu.VMEM((species, reactions), F32),
        pltpu.VMEM((species, reactions), F32),
        pltpu.VMEM((species, reactions), F32),
        pltpu.SemaphoreType.DMA,
        pltpu.SemaphoreType.DMA,
        pltpu.SemaphoreType.DMA((listed,)),
        pltpu.SemaphoreType.DMA((10,)),
    ]
    return kernel, scratch


def on_device(
    composition,
    heat_level,
    step_counts,
    burning_parcel_roster,
    target_compute_place,
    partial_reciprocal_operator,
    speed_log_prefactor,
    arrhenius_barrier,
    leading_ingredient,
    trailing_ingredient,
    molar_coefficients,
):
    blocks, species, cells = composition.shape
    reactions = speed_log_prefactor.shape[0]
    listed = burning_parcel_roster.shape[0]
    kernel, scratch = make_kernel(species, reactions, blocks, cells, listed)
    hbm = pl.BlockSpec(memory_space=pltpu.HBM)
    out = pl.pallas_call(
        kernel,
        out_shape=jax.ShapeDtypeStruct((species, blocks, cells), composition.dtype),
        in_specs=[hbm] * 11,
        out_specs=hbm,
        scratch_shapes=scratch,
        compiler_params=pltpu.CompilerParams(vmem_limit_bytes=67043328),
        name="integrate",
    )(
        jnp.transpose(composition, (1, 0, 2)),
        heat_level,
        step_counts,
        burning_parcel_roster,
        target_compute_place,
        partial_reciprocal_operator,
        speed_log_prefactor,
        arrhenius_barrier,
        leading_ingredient.T,
        trailing_ingredient.T,
        molar_coefficients,
    )
    return jnp.transpose(out, (1, 0, 2))


def solution(mesh):
    owners = tuple(mesh.axis_names)
    return jax.shard_map(
        on_device,
        mesh=mesh,
        in_specs=(
            P(owners, None, None),
            P(owners, None),
            P(owners),
            P(owners),
            P(owners),
            P(owners, None, None),
            P(),
            P(),
            P(),
            P(),
            P(),
        ),
        out_specs=P(owners, None, None),
        check_vma=False,
    )
```
